32 devices in a mesh: ga: 8 (over z, y), band: 4 (over x, core).
Axes of the slice: x: 2, y: 2, z: 4, core: 2. Of those that a mesh axis runs over, the one named last changes fastest.
Arguments:
- band_coeffs: bfloat16 [8192, 256], P('ga', 'band'), may hold values from -6 to 6
- beta_vectors: bfloat16 [8192, 2048], P('ga'), may hold values from -0.0625 to 0.0625
- atomic_waves: bfloat16 [8192, 1280], P('ga'), may hold values from -0.0625 to 0.0625
- beta_coupling: float32 [2048, 11], replicated, may hold values from -1 to 2
- ortho_inverse: bfloat16 [1280, 1280], replicated, may hold values from -1 to 2
- hubbard_energy: float32 [3], replicated, may hold values from 1 to 4
- band_weight: float32 [256], P('band'), may hold values from 0 to 0.015625
- orbital_start: int32 [1280], replicated, may hold values from 0 to 1277, as said below
- orbital_species: int32 [1280], replicated, may hold values from 0 to 2, as said below
- beta_start: int32 [2048], replicated, may hold values from 0 to 2046, as said below
Outputs:
- hubbard_apply: bfloat16 [8192, 256], P('ga', 'band')
The draws below stay inside these ranges and needn't reach their ends.
Inputs may be any that keep to these rules, and one draw needn't show every extreme that they name: `orbital_start`: every atom holds 3 or 5 consecutive orbitals; each orbital holds the index of its atom's first orbital. `orbital_species`: orbitals of 5-orbital atoms have species 0 or 1, orbitals of 3-orbital atoms species 2. `beta_start`: every atom holds 2 or 6 consecutive projectors; each projector holds the index of its atom's first projector.
All inputs are finite; a program needn't handle non-finite values.
Results may differ from the reference program's by a relative error of at most 0.0085.
Values sent between devices are 32-bit elements; how exact they have to be, the bound alone decides.
No kernel may reach another device: no remote copies, remote signals or barrier semaphores. Data moves between devices by JAX's collectives and lax.ppermute only.
A program may use at most 64 MiB of HBM per device.

```python
import jax
import jax.numpy as jnp
from jax import lax

NWFC = 1280
NBETA = 2048
ORB_REACH = 4
BETA_REACH = 5
NSPEC = 3
NPW = 8192
NBANDS = 256


def orbital_layout(key):
    groups = NWFC // 8
    flips = jax.random.randint(jax.random.fold_in(key, 11), (groups,), 0, 2)
    metals = jax.random.randint(jax.random.fold_in(key, 12), (groups,), 0, 2)
    first_size = jnp.where(flips == 0, 5, 3)
    place = jnp.arange(8, dtype=jnp.int32)[None, :]
    in_first = place < first_size[:, None]
    local = jnp.where(in_first, 0, first_size[:, None])
    starts = (jnp.arange(groups, dtype=jnp.int32) * 8)[:, None] + local
    own_size = jnp.where(in_first, first_size[:, None], 8 - first_size[:, None])
    species = jnp.where(own_size == 5, metals[:, None], 2)
    return (starts.reshape(-1).astype(jnp.int32), species.reshape(-1).astype(jnp.int32))


def draw_orbital_start(key, part):
    return orbital_layout(key)[0]


def draw_orbital_species(key, part):
    return orbital_layout(key)[1]


def draw_beta_start(key, part):
    groups = NBETA // 8
    flips = jax.random.randint(jax.random.fold_in(key, 21), (groups,), 0, 2)
    first_size = jnp.where(flips == 0, 6, 2)
    place = jnp.arange(8, dtype=jnp.int32)[None, :]
    local = jnp.where(place < first_size[:, None], 0, first_size[:, None])
    starts = (jnp.arange(groups, dtype=jnp.int32) * 8)[:, None] + local
    return starts.reshape(-1).astype(jnp.int32)


def draw_ortho_inverse(key, part):
    noise = jax.random.normal(jax.random.fold_in(key, 31), (NWFC, NWFC), jnp.float32)
    spread = 0.0085
    diagonal = jnp.ones((NWFC,), jnp.float32)
    return (jnp.diag(diagonal) + spread * (noise + noise.T) / 1.4142135).astype(jnp.bfloat16)


def draw_band_weight(key, part):
    position = jnp.arange(NBANDS, dtype=jnp.float32) / NBANDS
    factor = jax.random.uniform(jax.random.fold_in(key, 41), (NBANDS,), jnp.float32, 0.5, 1.0)
    return (4.0 - 3.0 * position) * factor / NBANDS


def levels(rng, dims, split, smallest, high):
    gain = 1.0
    for dim, shards_of in split:
        steps = jax.random.uniform(jax.random.fold_in(jax.random.fold_in(rng, 6), dim), (shards_of,), jnp.float32, smallest / len(split), high / len(split))
        gain = gain * jnp.repeat(jnp.exp(steps), dims[dim] // shards_of).reshape((-1,) + (1,) * (len(dims) - 1 - dim))
    return gain


def centred(stream_key, shape, scale, most, shards=(), kind=jnp.bfloat16):
    array = scale * jax.random.normal(stream_key, shape, jnp.float32)
    if shards:
        array = array * levels(stream_key, shape, shards, -0.22, 0.18)
    return jnp.clip(array, -most, most).astype(kind)


def setup_inputs(seed: int = 0) -> dict:
    keys = jax.random.split(jax.random.key(seed), 11)
    return {
        "band_coeffs": centred(keys[0], (NPW, NBANDS), 1.0, 6.0, ((0, 8), (1, 4))),
        "beta_vectors": centred(keys[1], (NPW, NBETA), NPW ** -0.5, 0.0625, ((0, 8),)),
        "atomic_waves": centred(keys[2], (NPW, NWFC), NPW ** -0.5, 0.0625, ((0, 8),)),
        "beta_coupling": jnp.clip(jax.random.uniform(keys[3], (NBETA, 2 * BETA_REACH + 1), jnp.float32, -1.0, 2.0), -1.0, 2.0),
        "ortho_inverse": draw_ortho_inverse(jax.random.fold_in(keys[10], 71), 0),
        "hubbard_energy": jnp.clip(jax.random.uniform(keys[5], (NSPEC,), jnp.float32, 1.0, 4.0), 1.0, 4.0),
        "band_weight": draw_band_weight(jax.random.fold_in(keys[10], 71), 0),
        "orbital_start": draw_orbital_start(jax.random.fold_in(keys[10], 71), 0),
        "orbital_species": draw_orbital_species(jax.random.fold_in(keys[10], 71), 0),
        "beta_start": draw_beta_start(jax.random.fold_in(keys[10], 71), 0),
    }


def rim_shift(extended, reach, offset, rows):
    return lax.slice_in_dim(extended, reach + offset, reach + offset + rows, axis=0)


def same_atom(start_ext, reach, rows):
    centre = rim_shift(start_ext, reach, 0, rows)
    return jnp.stack([(rim_shift(start_ext, reach, offset, rows) == centre).astype(jnp.float32) for offset in range(-reach, reach + 1)])


def band_apply(coupling, extended, reach, rows):
    total = jnp.zeros((rows, extended.shape[1]), jnp.float32)
    for offset in range(-reach, reach + 1):
        total = total + coupling[offset + reach][:, None] * rim_shift(extended, reach, offset, rows)
    return total


def beta_matrix(beta_coupling, beta_start):
    rows = beta_start.shape[0]
    start_ext = jnp.pad(beta_start, BETA_REACH, constant_values=-1)
    mask = same_atom(start_ext, BETA_REACH, rows)
    padded = jnp.pad(beta_coupling, ((BETA_REACH, BETA_REACH), (0, 0)))
    terms = []
    for offset in range(-BETA_REACH, BETA_REACH + 1):
        mirror = rim_shift(padded, BETA_REACH, offset, rows)[:, BETA_REACH - offset]
        terms.append(0.5 * (beta_coupling[:, BETA_REACH + offset] + mirror))
    return jnp.stack(terms) * mask


def occupancy(extended, weights, mask, reach, rows):
    centre = rim_shift(extended, reach, 0, rows)
    weighted = centre * weights[None, :]
    return jnp.stack([jnp.sum(weighted * rim_shift(extended, reach, offset, rows), axis=1) for offset in range(-reach, reach + 1)]) * mask


def hubbard_mix(occupied, u_rows, mask, extended, reach, rows):
    centre_flag = (jnp.arange(2 * reach + 1) == reach).astype(jnp.float32)[:, None]
    potential = u_rows[None, :] * (0.5 * centre_flag - occupied) * mask
    return band_apply(potential, extended, reach, rows)


def per_orbital_u(species, hubbard_energy):
    onehot = (species[:, None] == jnp.arange(NSPEC)[None, :]).astype(jnp.float32)
    return jnp.dot(onehot, hubbard_energy, precision=lax.Precision.HIGHEST)


def reference(band_coeffs, beta_vectors, atomic_waves, beta_coupling, ortho_inverse, hubbard_energy, band_weight, orbital_start, orbital_species, beta_start):
    highest = lax.Precision.HIGHEST
    ortho_full = ortho_inverse.astype(jnp.float32)
    coupling = beta_matrix(beta_coupling, beta_start)
    beta_correlation = jnp.dot(beta_vectors.T, band_coeffs, preferred_element_type=jnp.float32)
    corrected = band_apply(coupling, jnp.pad(beta_correlation, ((BETA_REACH, BETA_REACH), (0, 0))), BETA_REACH, NBETA).astype(jnp.bfloat16)
    correlation_psi = (band_coeffs.astype(jnp.float32) + jnp.dot(beta_vectors, corrected, preferred_element_type=jnp.float32)).astype(jnp.bfloat16)
    partial_sums = jnp.dot(atomic_waves.T, correlation_psi, preferred_element_type=jnp.float32)
    projections = jnp.dot(ortho_full, partial_sums, precision=highest)
    extended = jnp.pad(projections, ((ORB_REACH, ORB_REACH), (0, 0)))
    start_ext = jnp.pad(orbital_start, ORB_REACH, constant_values=-1)
    mask = same_atom(start_ext, ORB_REACH, NWFC)
    occupied = occupancy(extended, band_weight, mask, ORB_REACH, NWFC)
    u_full = per_orbital_u(orbital_species, hubbard_energy)
    mixed = hubbard_mix(occupied, u_full, mask, extended, ORB_REACH, NWFC)
    rotated = jnp.dot(ortho_full, mixed, precision=highest).astype(jnp.bfloat16)
    hubbard_waves = jnp.dot(atomic_waves, rotated, preferred_element_type=jnp.float32)
    wave_half = hubbard_waves.astype(jnp.bfloat16)
    beta_update = jnp.dot(beta_vectors.T, wave_half, preferred_element_type=jnp.float32)
    correction = band_apply(coupling, jnp.pad(beta_update, ((BETA_REACH, BETA_REACH), (0, 0))), BETA_REACH, NBETA).astype(jnp.bfloat16)
    return (hubbard_waves + jnp.dot(beta_vectors, correction, preferred_element_type=jnp.float32)).astype(jnp.bfloat16)
```

```python
import jax
import jax.numpy as jnp
from jax import lax
from jax.experimental import pallas as pl
from jax.experimental.pallas import tpu as pltpu
from jax.sharding import PartitionSpec as P

ORB_REACH = 4
BETA_REACH = 5
NSPEC = 3
QUAD = 4


def lane_shift(padded, reach, offset, cols):
    return lax.slice_in_dim(padded, reach + offset, reach + offset + cols, axis=-1)


def pad_lanes(values, reach, fill=0):
    pads = [(0, 0)] * (values.ndim - 1) + [(reach, reach)]
    return jnp.pad(values, pads, constant_values=fill)


def same_atom(start, reach):
    cols = start.shape[0]
    padded = pad_lanes(start, reach, -1)
    return jnp.stack(
        [
            (lane_shift(padded, reach, offset, cols) == start).astype(jnp.float32)
            for offset in range(-reach, reach + 1)
        ]
    )


def beta_matrix(beta_coupling, beta_start):
    cols = beta_start.shape[0]
    coupling = beta_coupling.T
    padded = pad_lanes(coupling, BETA_REACH)
    terms = []
    for offset in range(-BETA_REACH, BETA_REACH + 1):
        mirror = lane_shift(padded[BETA_REACH - offset], BETA_REACH, offset, cols)
        terms.append(0.5 * (coupling[BETA_REACH + offset] + mirror))
    return jnp.stack(terms) * same_atom(beta_start, BETA_REACH)


def exchange(values, axis, size, distance):
    return lax.ppermute(values, axis, [(i, i ^ distance) for i in range(size)])


def scatter_sum(values, axis, size):
    rows = values.shape[0] // QUAD
    got = [exchange(values[d * rows : (d + 1) * rows], axis, size, d) for d in range(1, QUAD)]
    total = values[:rows] + got[0] + got[1] + got[2]
    distance = QUAD
    while 2 * distance < size:
        total = total + exchange(total, axis, size, distance)
        distance *= 2
    if distance < size:
        return total, exchange(total, axis, size, distance)
    return total, jnp.zeros_like(total)


def gather_quad(part, axis, size):
    return [part] + [exchange(part, axis, size, d) for d in range(1, QUAD)]


def sum_parts(values, axis, size):
    distance = QUAD
    while distance < size:
        values = values + exchange(values, axis, size, distance)
        distance *= 2
    return gather_quad(values, axis, size)


def vmem_call(kernel, outs, *arrays):
    space = pl.BlockSpec(memory_space=pltpu.VMEM)
    return pl.pallas_call(
        kernel,
        in_specs=[space] * len(arrays),
        out_specs=jax.tree.map(lambda _: space, outs),
        out_shape=outs,
        name=kernel.__name__,
    )(*arrays)


def f32(*shape):
    return jax.ShapeDtypeStruct(shape, jnp.float32)


def bf16(*shape):
    return jax.ShapeDtypeStruct(shape, jnp.bfloat16)


def dot_nn(left, right):
    return lax.dot_general(
        left, right, (((1,), (0,)), ((), ())), preferred_element_type=jnp.float32
    )


def dot_nt(left, right):
    return lax.dot_general(
        left, right, (((1,), (1,)), ((), ())), preferred_element_type=jnp.float32
    )


def split_dot_nt(values, half_matrix):
    rows = values.shape[0]
    high = values.astype(jnp.bfloat16)
    low = (values - high.astype(jnp.float32)).astype(jnp.bfloat16)
    product = dot_nt(jnp.concatenate([high, low], axis=0), half_matrix)
    return product[:rows] + product[rows:]


def ahead(values, offset):
    cols = values.shape[1]
    shift = (-offset) % cols
    return pltpu.roll(values, shift, 1) if shift else values


def place_in_quad():
    return lax.rem(lax.axis_index("ga"), QUAD)


def project_kernel(coeffs_ref, beta_ref, ordered_ref, out_ref):
    step = pl.program_id(0)
    rows = ordered_ref.shape[0] // QUAD

    @pl.when(step == 0)
    def _():
        place = place_in_quad()
        turned = coeffs_ref[...].astype(jnp.float32).T.astype(jnp.bfloat16)
        for chunk in range(QUAD):
            start = pl.multiple_of(jnp.bitwise_xor(place, chunk) * rows, rows)
            ordered_ref[pl.ds(start, rows), :] = turned[chunk * rows : (chunk + 1) * rows]

    out_ref[...] = dot_nn(ordered_ref[...], beta_ref[...])


def project(coeffs, beta):
    grid_points, bands = coeffs.shape
    nbeta = beta.shape[1]
    tile = nbeta // 4
    return pl.pallas_call(
        project_kernel,
        grid=(nbeta // tile,),
        in_specs=[
            pl.BlockSpec((grid_points, bands), lambda i: (0, 0)),
            pl.BlockSpec((grid_points, tile), lambda i: (0, i)),
        ],
        out_specs=[
            pl.BlockSpec((bands, grid_points), lambda i: (0, 0)),
            pl.BlockSpec((bands, tile), lambda i: (0, i)),
        ],
        out_shape=[bf16(bands, grid_points), f32(bands, nbeta)],
        name="project",
    )(coeffs, beta)


def couple_kernel(near_ref, far_ref, coupling_ref, out_ref):
    values = near_ref[...] + far_ref[...]
    total = coupling_ref[BETA_REACH : BETA_REACH + 1, :] * values
    for offset in range(1, BETA_REACH + 1):
        for signed in (-offset, offset):
            row = BETA_REACH + signed
            total = total + coupling_ref[row : row + 1, :] * ahead(values, signed)
    out_ref[...] = total


def overlap_kernel(p0, p1, p2, p3, coeffs_ref, beta_ref, atomic_ref, out_ref):
    parts = [p[...].astype(jnp.bfloat16) for p in (p0, p1, p2, p3)]
    corrected = jnp.concatenate(parts, axis=0)
    psi = coeffs_ref[...].astype(jnp.float32) + dot_nt(corrected, beta_ref[...])
    out_ref[...] = dot_nn(psi.astype(jnp.bfloat16), atomic_ref[...])


def occupy_kernel(p0, p1, p2, p3, ortho_ref, weight_ref, proj_ref, out_ref):
    summed = jnp.concatenate([p[...] for p in (p0, p1, p2, p3)], axis=0)
    projections = split_dot_nt(summed, ortho_ref[...])
    proj_ref[...] = projections
    weighted = projections * weight_ref[...]
    out_ref[...] = jnp.zeros_like(out_ref)
    for offset in range(ORB_REACH + 1):
        pair = weighted * ahead(projections, offset)
        out_ref[offset : offset + 1, :] = jnp.sum(pair, axis=0, keepdims=True)


def apply_kernel(
    q0, q1, q2, q3, same_ref, energy_ref, proj_ref, ortho_ref, atomic_ref, beta_ref,
    waves_ref, out_ref,
):
    occupied = (q0[...] + q1[...] + q2[...] + q3[...]) * same_ref[...]
    energy = energy_ref[...]
    projections = proj_ref[...]
    mixed = energy * (0.5 - occupied[0:1]) * projections
    for offset in range(1, ORB_REACH + 1):
        pair = occupied[offset : offset + 1]
        mixed = mixed - (energy * pair) * ahead(projections, offset)
        mixed = mixed - (energy * ahead(pair, -offset)) * ahead(projections, -offset)
    rotated = split_dot_nt(mixed, ortho_ref[...]).astype(jnp.bfloat16)
    waves = dot_nt(rotated, atomic_ref[...])
    waves_ref[...] = waves
    out_ref[...] = dot_nn(waves.astype(jnp.bfloat16), beta_ref[...])


def finish_kernel(p0, p1, p2, p3, waves_ref, beta_ref, out_ref, ordered_ref):
    parts = [p[...].astype(jnp.bfloat16) for p in (p0, p1, p2, p3)]
    correction = jnp.concatenate(parts, axis=0)
    applied = waves_ref[...] + dot_nt(correction, beta_ref[...])
    place = place_in_quad()
    rows = applied.shape[0] // QUAD
    for chunk in range(QUAD):
        start = pl.multiple_of(jnp.bitwise_xor(place, chunk) * rows, rows)
        ordered_ref[pl.ds(start, rows), :] = applied[chunk * rows : (chunk + 1) * rows]
    out_ref[...] = ordered_ref[...].T.astype(jnp.bfloat16)


def finish(parts, waves, beta):
    bands, points = waves.shape
    space = pl.BlockSpec(memory_space=pltpu.VMEM)
    return pl.pallas_call(
        finish_kernel,
        in_specs=[space] * 6,
        out_specs=space,
        out_shape=bf16(points, bands),
        scratch_shapes=[pltpu.VMEM((bands, points), jnp.float32)],
        name="finish",
    )(*parts, waves, beta)


def ordered_weight(weight, place):
    chunks = weight.reshape(QUAD, -1)
    chunks = jnp.where((place & 1) == 1, chunks[jnp.array([1, 0, 3, 2])], chunks)
    chunks = jnp.where((place & 2) == 2, chunks[jnp.array([2, 3, 0, 1])], chunks)
    return chunks.reshape(-1, 1)


def shards(
    ga_size,
    band_size,
    band_coeffs,
    beta_vectors,
    atomic_waves,
    beta_coupling,
    ortho_inverse,
    hubbard_energy,
    band_weight,
    orbital_start,
    orbital_species,
    beta_start,
):
    bands = band_coeffs.shape[1]
    points, nbeta = beta_vectors.shape
    norbit = atomic_waves.shape[1]
    weight = ordered_weight(band_weight, place_in_quad())
    coupling = beta_matrix(beta_coupling, beta_start)
    same = same_atom(orbital_start, ORB_REACH)[ORB_REACH:]
    same = jnp.pad(same, ((0, 8 - same.shape[0]), (0, 0)))
    species = jnp.arange(NSPEC)[:, None] == orbital_species[None, :]
    energy = jnp.sum(jnp.where(species, hubbard_energy[:, None], 0.0), axis=0, keepdims=True)

    coeffs, correlation = project(band_coeffs, beta_vectors)
    near, far = scatter_sum(correlation, "ga", ga_size)
    part = vmem_call(couple_kernel, f32(*near.shape), near, far, coupling)
    corrected = gather_quad(part, "ga", ga_size)
    partial_sums = vmem_call(
        overlap_kernel, f32(bands, norbit), *corrected, coeffs, beta_vectors, atomic_waves
    )
    near, far = scatter_sum(partial_sums, "ga", ga_size)
    summed = gather_quad(near + far, "ga", ga_size)
    projections, occupied = vmem_call(
        occupy_kernel, (f32(bands, norbit), f32(8, norbit)), *summed, ortho_inverse, weight
    )
    occupied = sum_parts(occupied, "band", band_size)
    waves, update = vmem_call(
        apply_kernel,
        (f32(bands, points), f32(bands, nbeta)),
        *occupied,
        same,
        energy,
        projections,
        ortho_inverse,
        atomic_waves,
        beta_vectors,
    )
    near, far = scatter_sum(update, "ga", ga_size)
    part = vmem_call(couple_kernel, f32(*near.shape), near, far, coupling)
    correction = gather_quad(part, "ga", ga_size)
    return finish(correction, waves, beta_vectors)


def solution(mesh):
    sizes = dict(mesh.shape)
    placed = (
        P("ga", "band"),
        P("ga", None),
        P("ga", None),
        P(),
        P(),
        P(),
        P("band"),
        P(),
        P(),
        P(),
    )

    def body(*arrays):
        return shards(sizes["ga"], sizes["band"], *arrays)

    return jax.shard_map(
        body, mesh=mesh, in_specs=placed, out_specs=P("ga", "band"), check_vma=False
    )
```

```python
import jax
import jax.numpy as jnp
from jax import lax
from jax.experimental import pallas as pl
from jax.experimental.pallas import tpu as pltpu
from jax.sharding import PartitionSpec as P

ORB_REACH = 4
BETA_REACH = 5
NSPEC = 3
QUAD = 4


def exchange(values, axis, size, distance):
    return lax.ppermute(values, axis, [(i, i ^ distance) for i in range(size)])


def scatter_sum(chunks, axis, size):
    got = [exchange(chunks[d], axis, size, d) for d in range(1, QUAD)]
    total = add_all(chunks[0], *got)
    distance = QUAD
    while 2 * distance < size:
        total = add_all(total, exchange(total, axis, size, distance))
        distance *= 2
    if distance < size:
        return total, exchange(total, axis, size, distance)
    return total, jnp.zeros_like(total)


def gather_quad(part, axis, size):
    return [part] + [exchange(part, axis, size, d) for d in range(1, QUAD)]


def sum_parts(values, axis, size):
    distance = QUAD
    while distance < size:
        values = add_all(values, exchange(values, axis, size, distance))
        distance *= 2
    return gather_quad(values, axis, size)


def resident(array):
    return pltpu.with_memory_space_constraint(array, pltpu.VMEM)


def vmem_call(kernel, outs, *arrays, scratch=(), vmem=8 << 20):
    space = pl.BlockSpec(memory_space=pltpu.VMEM)
    return pl.pallas_call(
        kernel,
        in_specs=[space] * len(arrays),
        out_specs=[space] * len(outs),
        out_shape=outs,
        scratch_shapes=scratch,
        compiler_params=pltpu.CompilerParams(vmem_limit_bytes=vmem),
        name=kernel.__name__,
    )(*[resident(array) for array in arrays])


def f32(*shape):
    return pltpu.VMEM(shape, jnp.float32)


def bf16(*shape):
    return pltpu.VMEM(shape, jnp.bfloat16)


def sum_kernel(*refs):
    *in_refs, out_ref = refs
    total = in_refs[0][...]
    for ref in in_refs[1:]:
        total = total + ref[...]
    out_ref[...] = total


def add_all(*arrays):
    return vmem_call(sum_kernel, [f32(*arrays[0].shape)], *arrays)[0]


def dot_nn(left, right):
    return lax.dot_general(
        left, right, (((1,), (0,)), ((), ())), preferred_element_type=jnp.float32
    )


def dot_nt(left, right):
    return lax.dot_general(
        left, right, (((1,), (1,)), ((), ())), preferred_element_type=jnp.float32
    )


def split_dot_nt(values, half_matrix):
    rows = values.shape[0]
    high = values.astype(jnp.bfloat16)
    low = (values - high.astype(jnp.float32)).astype(jnp.bfloat16)
    product = dot_nt(jnp.concatenate([high, low], axis=0), half_matrix)
    return product[:rows] + product[rows:]


def ahead(values, offset):
    cols = values.shape[1]
    shift = (-offset) % cols
    return pltpu.roll(values, shift, 1) if shift else values


def place_in_quad():
    return lax.rem(lax.axis_index("ga"), QUAD)


def put_chunks(values, refs, columns=slice(None)):
    rows = values.shape[0] // QUAD
    for chunk, ref in enumerate(refs):
        ref[:, columns] = values[chunk * rows : (chunk + 1) * rows]


def project_kernel(coeffs_ref, beta_ref, ordered_ref, *out_refs):
    rows = ordered_ref.shape[0] // QUAD

    @pl.when(pl.program_id(0) == 0)
    def _():
        place = place_in_quad()
        for chunk in range(QUAD):
            start = pl.multiple_of(jnp.bitwise_xor(place, chunk) * rows, rows)
            ordered_ref[pl.ds(start, rows), :] = coeffs_ref[chunk * rows : (chunk + 1) * rows]

    put_chunks(dot_nn(ordered_ref[...], beta_ref[...]), out_refs)


def project(coeffs, beta):
    bands, points = coeffs.shape
    nbeta = beta.shape[1]
    tile = nbeta // 4
    rows = bands // QUAD
    return pl.pallas_call(
        project_kernel,
        grid=(nbeta // tile,),
        in_specs=[
            pl.BlockSpec((bands, points), lambda i: (0, 0)),
            pl.BlockSpec((points, tile), lambda i: (0, i)),
        ],
        out_specs=[pl.BlockSpec((bands, points), lambda i: (0, 0))]
        + [pl.BlockSpec((rows, tile), lambda i: (0, i))] * QUAD,
        out_shape=[bf16(bands, points)] + [f32(rows, nbeta)] * QUAD,
        compiler_params=pltpu.CompilerParams(vmem_limit_bytes=12 << 20),
        name="project",
    )(coeffs, beta)


def couple_kernel(near_ref, far_ref, coupling_ref, out_ref):
    values = near_ref[...] + far_ref[...]
    total = coupling_ref[BETA_REACH : BETA_REACH + 1, :] * values
    for offset in range(1, BETA_REACH + 1):
        for signed in (-offset, offset):
            row = BETA_REACH + signed
            total = total + coupling_ref[row : row + 1, :] * ahead(values, signed)
    out_ref[...] = total


def overlap_kernel(p0, p1, p2, p3, coeffs_ref, beta_ref, atomic_ref, *out_refs):
    parts = [p[...].astype(jnp.bfloat16) for p in (p0, p1, p2, p3)]
    corrected = jnp.concatenate(parts, axis=0)
    psi = coeffs_ref[...].astype(jnp.float32) + dot_nt(corrected, beta_ref[...])
    put_chunks(dot_nn(psi.astype(jnp.bfloat16), atomic_ref[...]), out_refs)


def occupy_kernel(p0, p1, p2, p3, ortho_ref, weight_ref, proj_ref, out_ref):
    summed = jnp.concatenate([p[...] for p in (p0, p1, p2, p3)], axis=0)
    projections = split_dot_nt(summed, ortho_ref[...])
    proj_ref[...] = projections
    weighted = projections * weight_ref[...]
    out_ref[...] = jnp.zeros_like(out_ref)
    for offset in range(ORB_REACH + 1):
        pair = weighted * ahead(projections, offset)
        out_ref[offset : offset + 1, :] = jnp.sum(pair, axis=0, keepdims=True)


def apply_kernel(
    q0, q1, q2, q3, same_ref, energy_ref, proj_ref, ortho_ref, atomic_ref, beta_ref,
    waves_ref, *out_refs,
):
    occupied = (q0[...] + q1[...] + q2[...] + q3[...]) * same_ref[...]
    energy = energy_ref[...]
    projections = proj_ref[...]
    mixed = energy * (0.5 - occupied[0:1]) * projections
    for offset in range(1, ORB_REACH + 1):
        pair = occupied[offset : offset + 1]
        mixed = mixed - (energy * pair) * ahead(projections, offset)
        mixed = mixed - (energy * ahead(pair, -offset)) * ahead(projections, -offset)
    rotated = split_dot_nt(mixed, ortho_ref[...]).astype(jnp.bfloat16)
    waves = dot_nt(rotated, atomic_ref[...])
    waves_ref[...] = waves
    put_chunks(dot_nn(waves.astype(jnp.bfloat16), beta_ref[...]), out_refs)


def finish_kernel(p0, p1, p2, p3, waves_ref, beta_ref, out_ref):
    parts = [p[...].astype(jnp.bfloat16) for p in (p0, p1, p2, p3)]
    correction = jnp.concatenate(parts, axis=0)
    applied = waves_ref[...] + dot_nt(correction, beta_ref[...])
    applied = applied.astype(out_ref.dtype)
    place = place_in_quad()
    rows = applied.shape[0] // QUAD
    for chunk in range(QUAD):
        start = pl.multiple_of(jnp.bitwise_xor(place, chunk) * rows, rows)
        out_ref[pl.ds(start, rows), :] = applied[chunk * rows : (chunk + 1) * rows]


def partner(start, offset, column):
    cols = start.shape[1]
    inside = (column + offset >= 0) & (column + offset < cols)
    return inside & (ahead(start, offset) == start)


def prepare_kernel(
    beta_coupling_ref, beta_start_ref, start_ref, species_ref, weight_ref, energy_ref,
    coupling_ref, same_ref, own_ref, column_ref,
):
    start = beta_start_ref[...]
    column = lax.broadcasted_iota(jnp.int32, start.shape, 1)
    for offset in range(-BETA_REACH, BETA_REACH + 1):
        here = beta_coupling_ref[BETA_REACH + offset : BETA_REACH + offset + 1, :]
        there = beta_coupling_ref[BETA_REACH - offset : BETA_REACH - offset + 1, :]
        value = jnp.where(
            partner(start, offset, column), 0.5 * (here + ahead(there, offset)), 0.0
        )
        coupling_ref[BETA_REACH + offset : BETA_REACH + offset + 1, :] = value
    start = start_ref[...]
    column = lax.broadcasted_iota(jnp.int32, start.shape, 1)
    same_ref[...] = jnp.zeros_like(same_ref)
    for offset in range(ORB_REACH + 1):
        same_ref[offset : offset + 1, :] = partner(start, offset, column).astype(jnp.float32)
    own = jnp.zeros(start.shape, jnp.float32)
    for kind in range(NSPEC):
        own = own + jnp.where(species_ref[...] == kind, energy_ref[kind], 0.0)
    own_ref[...] = own
    rows = column_ref.shape[0] // QUAD
    weight = jnp.broadcast_to(weight_ref[...], (rows, weight_ref.shape[1]))
    row = lax.broadcasted_iota(jnp.int32, weight.shape, 0)
    column = lax.broadcasted_iota(jnp.int32, weight.shape, 1)
    place = place_in_quad()
    for chunk in range(QUAD):
        source = row + jnp.bitwise_xor(place, chunk) * rows
        picked = jnp.sum(jnp.where(column == source, weight, 0.0), axis=1, keepdims=True)
        column_ref[chunk * rows : (chunk + 1) * rows, :] = picked


def prepare(beta_coupling, beta_start, orbital_start, orbital_species, band_weight, energy):
    space = pl.BlockSpec(memory_space=pltpu.VMEM)
    norbit = orbital_start.shape[0]
    outs = [
        f32(*beta_coupling.T.shape),
        f32(8, norbit),
        f32(1, norbit),
        f32(band_weight.shape[0], 1),
    ]
    return pl.pallas_call(
        prepare_kernel,
        in_specs=[space] * 5 + [pl.BlockSpec(memory_space=pltpu.SMEM)],
        out_specs=[space] * len(outs),
        out_shape=outs,
        compiler_params=pltpu.CompilerParams(vmem_limit_bytes=4 << 20),
        name="prepare",
    )(
        beta_coupling.T,
        beta_start[None, :],
        orbital_start[None, :],
        orbital_species[None, :],
        band_weight[None, :],
        energy,
    )


def shards(
    ga_size,
    band_size,
    band_coeffs,
    beta_vectors,
    atomic_waves,
    beta_coupling,
    ortho_inverse,
    hubbard_energy,
    band_weight,
    orbital_start,
    orbital_species,
    beta_start,
):
    bands = band_coeffs.shape[1]
    points, nbeta = beta_vectors.shape
    norbit = atomic_waves.shape[1]
    coupling, same, energy, weight = prepare(
        beta_coupling, beta_start, orbital_start, orbital_species, band_weight, hubbard_energy
    )
    rows = bands // QUAD
    coeffs, *correlation = project(band_coeffs.T, beta_vectors)
    near, far = scatter_sum(correlation, "ga", ga_size)
    (part,) = vmem_call(couple_kernel, [f32(rows, nbeta)], near, far, coupling)
    corrected = gather_quad(part, "ga", ga_size)
    partial_sums = vmem_call(
        overlap_kernel,
        [f32(rows, norbit)] * QUAD,
        *corrected,
        coeffs,
        beta_vectors,
        atomic_waves,
    )
    near, far = scatter_sum(partial_sums, "ga", ga_size)
    summed = gather_quad(add_all(near, far), "ga", ga_size)
    projections, occupied = vmem_call(
        occupy_kernel, [f32(bands, norbit), f32(8, norbit)], *summed, ortho_inverse, weight
    )
    occupied = sum_parts(occupied, "band", band_size)
    waves, *update = vmem_call(
        apply_kernel,
        [f32(bands, points)] + [f32(rows, nbeta)] * QUAD,
        *occupied,
        same,
        energy,
        projections,
        ortho_inverse,
        atomic_waves,
        beta_vectors,
    )
    near, far = scatter_sum(update, "ga", ga_size)
    (part,) = vmem_call(couple_kernel, [f32(rows, nbeta)], near, far, coupling)
    correction = gather_quad(part, "ga", ga_size)
    (applied,) = vmem_call(
        finish_kernel,
        [jax.ShapeDtypeStruct((bands, points), jnp.bfloat16)],
        *correction, waves, beta_vectors
    )
    return applied.T


def solution(mesh):
    sizes = dict(mesh.shape)
    placed = (
        P("ga", "band"),
        P("ga", None),
        P("ga", None),
        P(),
        P(),
        P(),
        P("band"),
        P(),
        P(),
        P(),
    )

    def body(*arrays):
        return shards(sizes["ga"], sizes["band"], *arrays)

    return jax.shard_map(
        body, mesh=mesh, in_specs=placed, out_specs=P("ga", "band"), check_vma=False
    )
```

```python
import jax
import jax.numpy as jnp
from jax import lax
from jax.experimental import pallas as pl
from jax.experimental.pallas import tpu as pltpu
from jax.sharding import PartitionSpec as P


ORB_REACH = 4
BETA_REACH = 5
NSPEC = 3
QUAD = 4
TILES = 4
START_ORDER = (2, 1, 3)


def exchange(values, axis, size, distance):
    return lax.ppermute(values, axis, [(i, i ^ distance) for i in range(size)])


def exchange_quad(chunks, axis, size):
    got = {}
    for d in START_ORDER:
        got[d] = exchange(chunks[d], axis, size, d)
    return [got[d] for d in range(1, QUAD)]


def scatter_sum(chunks, axis, size):
    got = exchange_quad(chunks, axis, size)
    total = add_all(chunks[0], *got)
    distance = QUAD
    while 2 * distance < size:
        total = add_all(total, exchange(total, axis, size, distance))
        distance *= 2
    if distance < size:
        return total, exchange(total, axis, size, distance)
    return total, jnp.zeros_like(total)


def gather_quad(part, axis, size):
    return [part] + exchange_quad([part] * QUAD, axis, size)


def sum_parts(values, axis, size):
    distance = QUAD
    while distance < size:
        values = add_all(values, exchange(values, axis, size, distance))
        distance *= 2
    return gather_quad(values, axis, size)


def resident(array):
    return pltpu.with_memory_space_constraint(array, pltpu.VMEM)


def in_hbm(array):
    return pltpu.with_memory_space_constraint(array, pltpu.HBM)


def vmem_call(kernel, outs, *arrays, scratch=(), vmem=8 << 20):
    space = pl.BlockSpec(memory_space=pltpu.VMEM)
    return pl.pallas_call(
        kernel,
        in_specs=[space] * len(arrays),
        out_specs=[space] * len(outs),
        out_shape=outs,
        scratch_shapes=scratch,
        compiler_params=pltpu.CompilerParams(vmem_limit_bytes=vmem),
    )(*[resident(array) for array in arrays])


def f32(*shape):
    return pltpu.VMEM(shape, jnp.float32)


def bf16(*shape):
    return pltpu.VMEM(shape, jnp.bfloat16)


def sum_kernel(*refs):
    *in_refs, out_ref = refs
    total = in_refs[0][...]
    for ref in in_refs[1:]:
        total = total + ref[...]
    out_ref[...] = total


def add_all(*arrays):
    return vmem_call(sum_kernel, [f32(*arrays[0].shape)], *arrays)[0]


def dot_nn(left, right):
    return lax.dot_general(
        left, right, (((1,), (0,)), ((), ())), preferred_element_type=jnp.float32
    )


def dot_nt(left, right):
    return lax.dot_general(
        left, right, (((1,), (1,)), ((), ())), preferred_element_type=jnp.float32
    )


def split_dot_nt(values, half_matrix):
    rows = values.shape[0]
    high = values.astype(jnp.bfloat16)
    low = (values - high.astype(jnp.float32)).astype(jnp.bfloat16)
    product = dot_nt(jnp.concatenate([high, low], axis=0), half_matrix)
    return product[:rows] + product[rows:]


def ahead(values, offset):
    cols = values.shape[1]
    shift = (-offset) % cols
    return pltpu.roll(values, shift, 1) if shift else values


def place_in_quad():
    return lax.rem(lax.axis_index("ga"), QUAD)


def put_chunks(values, refs, columns=slice(None)):
    rows = values.shape[0] // QUAD
    for chunk, ref in enumerate(refs):
        ref[:, columns] = values[chunk * rows : (chunk + 1) * rows]


def project_kernel(coeffs_ref, beta_ref, ordered_ref, kept_ref, *refs):
    *out_refs, sems = refs
    tile = beta_ref.shape[1] // TILES
    spans = [slice(i * tile, (i + 1) * tile) for i in range(TILES)]
    copies = []
    for i, span in enumerate(spans):
        copy = pltpu.make_async_copy(beta_ref.at[:, span], kept_ref.at[:, span], sems.at[i])
        copy.start()
        copies.append(copy)
    rows = ordered_ref.shape[0] // QUAD
    place = place_in_quad()
    for chunk in range(QUAD):
        start = pl.multiple_of(jnp.bitwise_xor(place, chunk) * rows, rows)
        ordered_ref[pl.ds(start, rows), :] = coeffs_ref[chunk * rows : (chunk + 1) * rows]
    for copy, span in zip(copies, spans):
        copy.wait()
        put_chunks(dot_nn(ordered_ref[...], kept_ref[:, span]), out_refs, span)


def project(coeffs, beta):
    bands, points = coeffs.shape
    nbeta = beta.shape[1]
    rows = bands // QUAD
    space = pl.BlockSpec(memory_space=pltpu.VMEM)
    outs = [bf16(bands, points), bf16(points, nbeta)] + [f32(rows, nbeta)] * QUAD
    return pl.pallas_call(
        project_kernel,
        in_specs=[space, pl.BlockSpec(memory_space=pltpu.HBM)],
        out_specs=[space] * len(outs),
        out_shape=outs,
        scratch_shapes=[pltpu.SemaphoreType.DMA((TILES,))],
        compiler_params=pltpu.CompilerParams(vmem_limit_bytes=4 << 20),
        name="project",
    )(in_hbm(coeffs), in_hbm(beta))


def turn_kernel(atomic_ref, coeffs_ref, turned_ref, seed_ref):
    turned_ref[...] = atomic_ref[...].T
    seed_ref[...] = dot_nn(coeffs_ref[...], atomic_ref[...])


def gram_kernel(span, turned_ref, beta_ref, after_ref, out_ref):
    out_ref[...] = dot_nn(turned_ref[...], beta_ref[:, span]).astype(out_ref.dtype)


def gram(index, turned, beta, after):
    norbit, nbeta = turned.shape[0], beta.shape[1]
    tile = nbeta // TILES
    space = pl.BlockSpec(memory_space=pltpu.VMEM)

    def kernel(*refs):
        gram_kernel(slice(index * tile, (index + 1) * tile), *refs)

    return pl.pallas_call(
        kernel,
        in_specs=[space, space, pl.BlockSpec(memory_space=pl.ANY)],
        out_specs=space,
        out_shape=bf16(norbit, tile),
        compiler_params=pltpu.CompilerParams(vmem_limit_bytes=8 << 20),
        name="gram",
    )(resident(turned), resident(beta), resident(after))


def couple_kernel(near_ref, far_ref, coupling_ref, out_ref):
    values = near_ref[...] + far_ref[...]
    total = coupling_ref[BETA_REACH : BETA_REACH + 1, :] * values
    for offset in range(1, BETA_REACH + 1):
        for signed in (-offset, offset):
            row = BETA_REACH + signed
            total = total + coupling_ref[row : row + 1, :] * ahead(values, signed)
    out_ref[...] = total


def overlap_kernel(p0, p1, p2, p3, seed_ref, *refs):
    gram_refs, out_refs = refs[:TILES], refs[TILES:]
    parts = [p[...].astype(jnp.bfloat16) for p in (p0, p1, p2, p3)]
    corrected = jnp.concatenate(parts, axis=0)
    total = seed_ref[...]
    tile = gram_refs[0].shape[1]
    for i, ref in enumerate(gram_refs):
        total = total + dot_nt(corrected[:, i * tile : (i + 1) * tile], ref[...])
    put_chunks(total, out_refs)


def occupy_kernel(p0, p1, p2, p3, ortho_ref, weight_ref, proj_ref, out_ref):
    summed = jnp.concatenate([p[...] for p in (p0, p1, p2, p3)], axis=0)
    projections = split_dot_nt(summed, ortho_ref[...])
    proj_ref[...] = projections
    weighted = projections * weight_ref[...]
    out_ref[...] = jnp.zeros_like(out_ref)
    for offset in range(ORB_REACH + 1):
        pair = weighted * ahead(projections, offset)
        out_ref[offset : offset + 1, :] = jnp.sum(pair, axis=0, keepdims=True)


def apply_kernel(
    q0, q1, q2, q3, same_ref, energy_ref, proj_ref, ortho_ref, *refs,
):
    gram_refs, rotated_ref, out_refs = refs[:TILES], refs[TILES], refs[TILES + 1 :]
    occupied = (q0[...] + q1[...] + q2[...] + q3[...]) * same_ref[...]
    energy = energy_ref[...]
    projections = proj_ref[...]
    mixed = energy * (0.5 - occupied[0:1]) * projections
    for offset in range(1, ORB_REACH + 1):
        pair = occupied[offset : offset + 1]
        mixed = mixed - (energy * pair) * ahead(projections, offset)
        mixed = mixed - (energy * ahead(pair, -offset)) * ahead(projections, -offset)
    rotated = split_dot_nt(mixed, ortho_ref[...]).astype(jnp.bfloat16)
    rotated_ref[...] = rotated
    tile = gram_refs[0].shape[1]
    for i, ref in enumerate(gram_refs):
        put_chunks(dot_nn(rotated, ref[...]), out_refs, slice(i * tile, (i + 1) * tile))


def waves_kernel(rotated_ref, turned_ref, out_ref):
    out_ref[...] = dot_nn(rotated_ref[...], turned_ref[...])


def finish_kernel(p0, p1, p2, p3, waves_ref, beta_ref, out_ref):
    parts = [p[...].astype(jnp.bfloat16) for p in (p0, p1, p2, p3)]
    correction = jnp.concatenate(parts, axis=0)
    applied = waves_ref[...] + dot_nt(correction, beta_ref[...])
    applied = applied.astype(out_ref.dtype)
    place = place_in_quad()
    rows = applied.shape[0] // QUAD
    for chunk in range(QUAD):
        start = pl.multiple_of(jnp.bitwise_xor(place, chunk) * rows, rows)
        out_ref[pl.ds(start, rows), :] = applied[chunk * rows : (chunk + 1) * rows]


def partner(start, offset, column):
    cols = start.shape[1]
    inside = (column + offset >= 0) & (column + offset < cols)
    return inside & (ahead(start, offset) == start)


def prepare_kernel(
    beta_coupling_ref, beta_start_ref, start_ref, species_ref, weight_ref, energy_ref,
    coupling_ref, same_ref, own_ref, column_ref,
):
    start = beta_start_ref[...]
    column = lax.broadcasted_iota(jnp.int32, start.shape, 1)
    for offset in range(-BETA_REACH, BETA_REACH + 1):
        here = beta_coupling_ref[BETA_REACH + offset : BETA_REACH + offset + 1, :]
        there = beta_coupling_ref[BETA_REACH - offset : BETA_REACH - offset + 1, :]
        value = jnp.where(
            partner(start, offset, column), 0.5 * (here + ahead(there, offset)), 0.0
        )
        coupling_ref[BETA_REACH + offset : BETA_REACH + offset + 1, :] = value
    start = start_ref[...]
    column = lax.broadcasted_iota(jnp.int32, start.shape, 1)
    same_ref[...] = jnp.zeros_like(same_ref)
    for offset in range(ORB_REACH + 1):
        same_ref[offset : offset + 1, :] = partner(start, offset, column).astype(jnp.float32)
    own = jnp.zeros(start.shape, jnp.float32)
    for kind in range(NSPEC):
        own = own + jnp.where(species_ref[...] == kind, energy_ref[kind], 0.0)
    own_ref[...] = own
    rows = column_ref.shape[0] // QUAD
    weight = jnp.broadcast_to(weight_ref[...], (rows, weight_ref.shape[1]))
    row = lax.broadcasted_iota(jnp.int32, weight.shape, 0)
    column = lax.broadcasted_iota(jnp.int32, weight.shape, 1)
    place = place_in_quad()
    for chunk in range(QUAD):
        source = row + jnp.bitwise_xor(place, chunk) * rows
        picked = jnp.sum(jnp.where(column == source, weight, 0.0), axis=1, keepdims=True)
        column_ref[chunk * rows : (chunk + 1) * rows, :] = picked


def prepare(beta_coupling, beta_start, orbital_start, orbital_species, band_weight, energy):
    space = pl.BlockSpec(memory_space=pltpu.VMEM)
    norbit = orbital_start.shape[0]
    outs = [
        f32(*beta_coupling.T.shape),
        f32(8, norbit),
        f32(1, norbit),
        f32(band_weight.shape[0], 1),
    ]
    return pl.pallas_call(
        prepare_kernel,
        in_specs=[space] * 5 + [pl.BlockSpec(memory_space=pltpu.SMEM)],
        out_specs=[space] * len(outs),
        out_shape=outs,
        compiler_params=pltpu.CompilerParams(vmem_limit_bytes=4 << 20),
        name="prepare",
    )(
        beta_coupling.T,
        beta_start[None, :],
        orbital_start[None, :],
        orbital_species[None, :],
        band_weight[None, :],
        energy,
    )


def shards(
    ga_size,
    band_size,
    band_coeffs,
    beta_vectors,
    atomic_waves,
    beta_coupling,
    ortho_inverse,
    hubbard_energy,
    band_weight,
    orbital_start,
    orbital_species,
    beta_start,
):
    bands = band_coeffs.shape[1]
    points, nbeta = beta_vectors.shape
    norbit = atomic_waves.shape[1]
    coupling, same, energy, weight = prepare(
        beta_coupling, beta_start, orbital_start, orbital_species, band_weight, hubbard_energy
    )
    rows = bands // QUAD
    coeffs, beta, *correlation = project(band_coeffs.T, beta_vectors)
    atomic, ortho, _ = lax.optimization_barrier((atomic_waves, ortho_inverse, correlation[0]))
    turned, seed = vmem_call(
        turn_kernel, [bf16(norbit, points), f32(bands, norbit)], atomic, coeffs
    )
    grams = [gram(i, turned, beta, correlation[0]) for i in range(2)]
    near, far = scatter_sum(correlation, "ga", ga_size)
    grams.append(gram(2, turned, beta, near))
    (part,) = vmem_call(couple_kernel, [f32(rows, nbeta)], near, far, coupling)
    corrected = gather_quad(part, "ga", ga_size)
    grams.append(gram(3, turned, beta, part))
    partial_sums = vmem_call(
        overlap_kernel, [f32(rows, norbit)] * QUAD, *corrected, seed, *grams
    )
    near, far = scatter_sum(partial_sums, "ga", ga_size)
    summed = gather_quad(add_all(near, far), "ga", ga_size)
    projections, occupied = vmem_call(
        occupy_kernel, [f32(bands, norbit), f32(8, norbit)], *summed, ortho, weight
    )
    occupied = sum_parts(occupied, "band", band_size)
    rotated, *update = vmem_call(
        apply_kernel,
        [bf16(bands, norbit)] + [f32(rows, nbeta)] * QUAD,
        *occupied,
        same,
        energy,
        projections,
        ortho,
        *grams,
    )
    (waves,) = vmem_call(waves_kernel, [f32(bands, points)], rotated, turned)
    near, far = scatter_sum(update, "ga", ga_size)
    (part,) = vmem_call(couple_kernel, [f32(rows, nbeta)], near, far, coupling)
    correction = gather_quad(part, "ga", ga_size)
    (applied,) = vmem_call(
        finish_kernel,
        [jax.ShapeDtypeStruct((bands, points), jnp.bfloat16)],
        *correction,
        waves,
        beta,
    )
    return applied.T


def solution(mesh):
    sizes = dict(mesh.shape)
    placed = (
        P("ga", "band"),
        P("ga", None),
        P("ga", None),
        P(),
        P(),
        P(),
        P("band"),
        P(),
        P(),
        P(),
    )

    def body(*arrays):
        return shards(sizes["ga"], sizes["band"], *arrays)

    return jax.shard_map(
        body, mesh=mesh, in_specs=placed, out_specs=P("ga", "band"), check_vma=False
    )
```
